32 devices in a mesh: row: 8 (over z, y), col: 4 (over x, core).
Axes of the slice: x: 2, y: 2, z: 4, core: 2. Of those that a mesh axis runs over, the one named last changes fastest.
Arguments:
- momentum: float32 [8192, 8192], P('row', 'col'), may hold values from -6 to 6
- gradient: bfloat16 [8192, 8192], P('row', 'col'), may hold values from -6 to 6
- weight: bfloat16 [8192, 8192], P('row', 'col'), may hold values from -6 to 6
- right_start: float32 [8192, 512], P('col', 'row'), may hold values from -0.0625 to 0.0625
Outputs:
- new_momentum: float32 [8192, 8192], P('row', 'col')
- new_weight: bfloat16 [8192, 8192], P('row', 'col')
- new_right: float32 [8192, 512], P('col', 'row')
The draws below stay inside these ranges and needn't reach their ends.
All inputs are finite; a program needn't handle non-finite values.
Results may differ from the reference program's by a relative error of at most 0.001.
Values sent between devices are 32-bit elements; how exact they have to be, the bound alone decides.
A program may use at most 128 MiB of HBM per device.

```python
import jax
import jax.numpy as jnp
from jax import lax

OUT_DIM = 8192
IN_DIM = 8192
RANK = 512
ITERS = 2


def levels(key, dims, shards, least, top_value):
    loudness = 1.0
    for axis_at, blocks in shards:
        steps = jax.random.uniform(jax.random.fold_in(jax.random.fold_in(key, 6), axis_at), (blocks,), jnp.float32, least / len(shards), top_value / len(shards))
        loudness = loudness * jnp.repeat(jnp.exp(steps), dims[axis_at] // blocks).reshape((-1,) + (1,) * (len(dims) - 1 - axis_at))
    return loudness


def noise(key, dims, spread, most, split=(), held_as=jnp.bfloat16):
    factor_of = levels(key, dims, split, -0.22, 0.18) if split else 1.0
    result = jax.random.normal(key, dims, jnp.float32) * spread * factor_of
    return jnp.minimum(jnp.maximum(result, -most), most).astype(held_as)


def setup_inputs(seed: int = 0) -> dict:
    arg_keys = jax.random.split(jax.random.key(seed), 5)
    return {
        "momentum": noise(arg_keys[0], (OUT_DIM, IN_DIM), 1.0, 6.0, ((0, 8), (1, 4)), jnp.float32),
        "gradient": noise(arg_keys[1], (OUT_DIM, IN_DIM), 1.0, 6.0, ((0, 8), (1, 4))),
        "weight": noise(arg_keys[2], (OUT_DIM, IN_DIM), 1.0, 6.0, ((0, 8), (1, 4))),
        "right_start": noise(arg_keys[3], (IN_DIM, RANK), IN_DIM ** -0.5, 0.0625, ((0, 4), (1, 8)), jnp.float32),
    }


precise_mode = lax.Precision.HIGHEST
momentum_decay = 0.9
step_rate = 0.1
epsilon = 1e-06

def orthonormal(partials):
    gram_sum = jnp.dot(partials.T, partials, precision=precise_mode)
    triangle = jnp.linalg.cholesky(gram_sum)
    return jax.scipy.linalg.solve_triangular(triangle, partials.T, lower=True).T

def reference(momentum, gradient, weight, right_start):
    blended = momentum + gradient.astype(jnp.float32)
    right_factor = right_start
    for iteration in range(ITERS):
        left_rows = orthonormal(jnp.dot(blended, right_factor, precision=precise_mode))
        products = jnp.dot(left_rows.T, blended, precision=precise_mode).T
        col_norms = jnp.sqrt(lax.optimization_barrier(jnp.sum(products * products, axis=0, keepdims=True)) + epsilon)
        right_factor = products / col_norms
    new_momentum = blended - (1.0 - momentum_decay) * jnp.dot(left_rows, products.T, precision=precise_mode)
    scale_factor = step_rate * (OUT_DIM * IN_DIM / RANK) ** 0.5
    update = jnp.dot(left_rows, right_factor.T, precision=precise_mode)
    new_weight = (weight.astype(jnp.float32) - scale_factor * update).astype(jnp.bfloat16)
    return (new_momentum, new_weight, right_factor)
```

```python
import jax
import jax.numpy as jnp
from jax import lax
from jax.sharding import PartitionSpec as P

ITERS = 2
BLOCK = 128


gram_mode = lax.Precision.HIGHEST
wide_mode = lax.Precision.HIGH
momentum_decay = 0.9
step_rate = 0.1
epsilon = 1e-06


def self_gram(rows):
    return lax.dot_general(rows, rows, (((0,), (0,)), ((), ())), precision=gram_mode)


def times_transposed(a, b):
    return lax.dot_general(a, b, (((1,), (1,)), ((), ())), precision=gram_mode)


def solve_rows(rows, gram_sum):
    rank = gram_sum.shape[0]
    block = min(BLOCK, rank)
    trailing = gram_sum
    rest = rows
    solved = []
    for at in range(0, rank, block):
        size = min(block, rank - at)
        corner = lax.linalg.cholesky(trailing[:size, :size], symmetrize_input=False)
        inverse = lax.linalg.triangular_solve(
            corner, jnp.eye(size, dtype=corner.dtype), left_side=True, lower=True
        )
        block_rows = times_transposed(rest[:, :size], inverse)
        solved.append(block_rows)
        if at + size < rank:
            panel = times_transposed(trailing[size:, :size], inverse)
            trailing = trailing[size:, size:] - times_transposed(panel, panel)
            rest = rest[:, size:] - times_transposed(block_rows, panel)
    return jnp.concatenate(solved, axis=1)


def shards(momentum, gradient, weight, right_start):
    rows_at, cols_at = lax.psum(1, "row"), lax.psum(1, "col")
    out_dim, in_dim = momentum.shape[0] * rows_at, momentum.shape[1] * cols_at
    rank = right_start.shape[1] * rows_at
    blended = momentum + gradient.astype(jnp.float32)
    right_full = lax.all_gather(right_start, "row", axis=1, tiled=True)
    right_shard = right_start
    for iteration in range(ITERS):
        partials = jnp.dot(blended, right_full, precision=wide_mode)
        left_sum = lax.psum(partials, "col")
        gram_sum = lax.psum(self_gram(left_sum), "row")
        left_rows = solve_rows(left_sum, gram_sum)
        transposed = lax.dot_general(
            blended, left_rows, (((0,), (0,)), ((), ())), precision=wide_mode
        )
        products = lax.psum_scatter(transposed, "row", scatter_dimension=1, tiled=True)
        squares = lax.psum(jnp.sum(products * products, axis=0, keepdims=True), "col")
        col_norms = jnp.sqrt(squares + epsilon)
        right_shard = products / col_norms
        products_full, norms_full = (
            lax.all_gather(products, "row", axis=1, tiled=True),
            lax.all_gather(col_norms, "row", axis=1, tiled=True),
        )
        right_full = products_full / norms_full
    outer_dims = (((1,), (1,)), ((), ()))
    feedback = lax.dot_general(left_rows, products_full, outer_dims, precision=wide_mode)
    new_momentum = blended - (1.0 - momentum_decay) * feedback
    scale_factor = step_rate * (out_dim * in_dim / rank) ** 0.5
    update = lax.dot_general(left_rows, right_full, outer_dims, precision=wide_mode)
    new_weight = (weight.astype(jnp.float32) - scale_factor * update).astype(jnp.bfloat16)
    return (new_momentum, new_weight, right_shard)


def solution(mesh):
    return jax.shard_map(
        shards,
        mesh=mesh,
        in_specs=(P("row", "col"), P("row", "col"), P("row", "col"), P("col", "row")),
        out_specs=(P("row", "col"), P("row", "col"), P("col", "row")),
        check_vma=False,
    )
```
